32 devices in a mesh: band: 16 (over z, y, core), grid: 2 (over x).
Axes of the slice: x: 2, y: 2, z: 4, core: 2. Of those that a mesh axis runs over, the one named last changes fastest.
Arguments:
- orbitals: float32 [32, 48, 2304], P('band', 'grid'), may hold values from -6 to 6
- occupation: float32 [32], P('band'), may hold values from 0.2 to 1
Outputs:
- exchange: float32 [32, 48, 2304], P('band', 'grid')
The draws below stay inside these ranges and needn't reach their ends.
All inputs are finite; a program needn't handle non-finite values.
Results may differ from the reference program's by a relative error of at most 0.0003.
Values sent between devices are 32-bit elements; how exact they have to be, the bound alone decides.
A program may use at most 64 MiB of HBM per device.

```python
import jax
import jax.numpy as jnp
from jax import lax

GX = 48
GY = 48
GZ = 48
ORB_DEV = 2
STOPS = 3
ORBITALS = 32
N_BAND = 16


def block_levels(key, extent, cuts, least, high):
    def one(position, parts):
        draws = jax.random.uniform(jax.random.fold_in(jax.random.fold_in(key, 6), position), (parts,), jnp.float32, least / len(cuts), high / len(cuts))
        return jnp.repeat(jnp.exp(draws), extent[position] // parts).reshape((-1,) + (1,) * (len(extent) - position - 1))

    factor_of = one(*cuts[0])
    for cut in cuts[1:]:
        factor_of = factor_of * one(*cut)
    return factor_of


def normal_values(stream_key, extent, deviation, bound, cuts=(), kind=jnp.bfloat16):
    array = jax.random.normal(stream_key, extent, jnp.float32) * deviation
    if len(cuts) > 0:
        array = block_levels(stream_key, extent, cuts, -0.22, 0.18) * array
    return jnp.clip(array, min=-bound, max=bound).astype(kind)


def setup_inputs(seed: int = 0) -> dict:
    streams_of = jax.random.split(jax.random.key(seed), 3)
    orbitals = normal_values(streams_of[0], (ORBITALS, GX, GY * GZ), 1.0, 6.0, ((0, 16), (1, 2)), jnp.float32)
    occupation = jnp.clip(0.2 + 0.8 * jax.random.uniform(streams_of[1], (ORBITALS,), jnp.float32) ** block_levels(streams_of[1], (ORBITALS,), ((0, 16),), -0.2, 0.2), 0.2, 1.0)
    return dict(orbitals=orbitals, occupation=occupation)


def signed_square(length, count):
    index = jnp.arange(count, dtype=jnp.int32)
    signed = jnp.where(index <= length // 2, index, index - length)
    return (signed * signed).astype(jnp.float32)


def make_kernel():
    total = (signed_square(GX, GX)[:, None, None] + signed_square(GY, GY)[None, :, None]
             + signed_square(GZ, GZ // 2 + 1)[None, None, :])
    safe = jnp.where(total > 0, total, jnp.ones_like(total))
    return jnp.where(total > 0, (24.0 * 24.0 / jnp.pi) / safe, jnp.zeros_like(total))


def reference(orbitals, occupation):
    psi = orbitals.reshape(N_BAND, ORB_DEV, GX, GY, GZ)
    occ = occupation.reshape(N_BAND, ORB_DEV)
    kernel = make_kernel()

    def one_block(block):
        visit = lax.dynamic_index_in_dim(psi, block, 0, keepdims=False)
        total = jnp.zeros((ORB_DEV, GX, GY, GZ), jnp.float32)
        for stop in range(STOPS):
            other = ((block + stop) % N_BAND).astype(jnp.int32)
            own = lax.dynamic_index_in_dim(psi, other, 0, keepdims=False)
            weight = lax.dynamic_index_in_dim(occ, other, 0, keepdims=False)
            dens = own[:, None] * visit[None]
            spectrum = jnp.fft.rfftn(dens, axes=(2, 3, 4)) * kernel
            pot = jnp.fft.irfftn(spectrum, s=(GX, GY, GZ), axes=(2, 3, 4)).astype(jnp.float32)
            weighted = own * weight[:, None, None, None]
            total = total - 0.25 * jnp.einsum('ijxyz,ixyz->jxyz', pot, weighted,
                                              precision=lax.Precision.HIGHEST)
        return total

    out = lax.map(one_block, jnp.arange(N_BAND, dtype=jnp.int32))
    return out.reshape(ORBITALS, GX, GY * GZ).astype(jnp.float32)
```

```python
import jax
import jax.numpy as jnp
import numpy as np
from jax import lax
from jax.experimental import pallas as pl
from jax.experimental.pallas import tpu as pltpu
from jax.sharding import PartitionSpec as P

N = 48
HALF = N // 2
PLANE = N * N
COLS = PLANE // 2
STOPS = 3
CUTS = [(0, 256), (256, 256), (512, 256), (768, 256), (1024, 128)]


def cas(product, length):
    angle = (product % length) * (2.0 * np.pi / length)
    return np.cos(angle) + np.sin(angle)


def tables():
    i, h = np.arange(N), np.arange(HALF)
    along_z = np.tile(cas(i[:, None] * i[None, :], N), (1, HALF))
    even = cas(2 * h[:, None] * h[None, :], N)
    odd = cas(h[:, None] * (2 * h[None, :] + 1), N)
    along_y = np.stack([np.repeat(m, N, axis=1) for m in (even, odd, odd.T)])
    along_x = cas(i[:, None] * i[None, :], N)
    square = np.where(i <= HALF, i, i - N).astype(np.float64) ** 2
    order = np.concatenate([i[0::2], i[1::2]])
    total = square[:, None, None] + square[order][None, :, None] + square[None, None, :]
    coulomb = np.where(total > 0, 24.0 * 24.0 / np.pi / np.where(total > 0, total, 1.0), 0.0)
    coulomb = coulomb.reshape(N, PLANE) * (-0.25 / N**3)
    x_high = along_x.astype(np.float32).astype(jnp.bfloat16)
    x_low = (along_x - x_high.astype(np.float64)).astype(np.float32).astype(jnp.bfloat16)
    along_x = np.concatenate([x_high, x_high, x_low], axis=1)
    return (
        along_z.astype(np.float32),
        along_y.astype(np.float32),
        along_x,
        coulomb.astype(np.float32),
    )


def split(value):
    high = value.astype(jnp.bfloat16)
    return high, (value - high.astype(jnp.float32)).astype(jnp.bfloat16)


def dot(a, b):
    return jnp.dot(a, b, preferred_element_type=jnp.float32)


def build(along_z, along_y, w_high, w_low):
    for m in range(3):

        @pl.loop(0, HALF)
        def _(y):
            rows = pl.ds(pl.multiple_of(y * N, 16), N)
            high, low = split(along_z[...] * along_y[m, pl.ds(y, 1), :])
            w_high[m, rows, :] = high
            w_low[m, rows, :] = low


def pairs(mine, visits, acc, along_x, coulomb, w_high, w_low, lhs, xrhs):
    for p in range(2):
        hi, lo = slice(p * N, (p + 1) * N), slice((p + 2) * N, (p + 3) * N)
        for start in range(0, COLS, 128):
            left, right = slice(start, start + 128), slice(COLS + start, COLS + start + 128)
            first = mine(left) * visits(p, left)
            second = mine(right) * visits(p, right)
            for parity, value in enumerate((first + second, first - second)):
                lhs[parity, hi, left], lhs[parity, lo, left] = split(value)

    def yz(which, parity, cut):
        both = dot(lhs[parity], w_high[which, :, cut])
        return both[: 2 * N] + both[2 * N :] + dot(lhs[parity, : 2 * N, :], w_low[which, :, cut])

    for parity in range(2):
        for start, size in CUTS:
            value = yz(parity, parity, slice(start, start + size))
            high, low = split(value)
            to = slice(parity * COLS + start, parity * COLS + start + size)
            for p in range(2):
                rows = slice(p * N, (p + 1) * N)
                xrhs[p, :N, to] = high[rows]
                xrhs[p, N : 2 * N, to] = low[rows]
                xrhs[p, 2 * N :, to] = high[rows]
    for parity in range(2):
        for start, size in CUTS:
            at = slice(parity * COLS + start, parity * COLS + start + size)
            for p in range(2):
                work = dot(along_x[...], xrhs[p, :, at]) * coulomb[:, at]
                high, low = split(work)
                work = dot(along_x[...], jnp.concatenate([high, low, high], axis=0))
                high, low = split(work)
                lhs[parity, p * N : (p + 1) * N, start : start + size] = high
                lhs[parity, (p + 2) * N : (p + 3) * N, start : start + size] = low
    for start, size in CUTS:
        left, right = slice(start, start + size), slice(COLS + start, COLS + start + size)
        even, odd = yz(0, 0, left), yz(2, 1, left)
        for at, value in ((left, even + odd), (right, even - odd)):
            acc[:, at] += value[:N] * visits(0, at) + value[N:] * visits(1, at)


def kernel(mine_ref, visit_ref, along_z, along_y, along_x, coulomb, out, w_high, w_low, lhs, xrhs):
    build(along_z, along_y, w_high, w_low)
    out[...] = jnp.zeros_like(out)

    @pl.loop(0, STOPS)
    def _(stop):
        pairs(
            lambda at: mine_ref[:, at],
            lambda p, at: visit_ref[stop * 2 + p, :, at],
            out, along_x, coulomb, w_high, w_low, lhs, xrhs,
        )


def per_device(orbitals, occupation):
    count, slab, plane = orbitals.shape
    root = jnp.sqrt(occupation)
    devices = lax.axis_size("band")
    place = lax.axis_index("grid")
    route = [((i + 1) % devices, i) for i in range(devices)]
    block = lax.all_gather(orbitals * root[:, None, None], "grid", axis=1, tiled=True)
    blocks = [block]
    for _ in range(1, STOPS):
        blocks.append(lax.ppermute(blocks[-1], "band", route))
    mine = lax.dynamic_index_in_dim(block, place, 0, keepdims=False)
    scale = 1.0 / lax.dynamic_index_in_dim(root, place, 0, keepdims=False)
    vmem = pl.BlockSpec(memory_space=pltpu.VMEM)
    result = pl.pallas_call(
        kernel,
        out_shape=jax.ShapeDtypeStruct((N, plane), jnp.float32),
        in_specs=[vmem] * 6,
        out_specs=vmem,
        scratch_shapes=[
            pltpu.VMEM((3, COLS, COLS), jnp.bfloat16),
            pltpu.VMEM((3, COLS, COLS), jnp.bfloat16),
            pltpu.VMEM((2, 4 * N, COLS), jnp.bfloat16),
            pltpu.VMEM((2, 3 * N, PLANE), jnp.bfloat16),
        ],
        compiler_params=pltpu.CompilerParams(vmem_limit_bytes=50 << 20),
    )(mine, jnp.concatenate(blocks), *[jnp.asarray(t) for t in tables()])
    result = (result * scale).reshape(2, 1, slab, plane)
    result = lax.all_to_all(result, "grid", 0, 1)
    return result.reshape(count, slab, plane)


def solution(mesh):
    placed = (P("band", "grid", None), P("band"))
    return jax.shard_map(
        per_device, mesh=mesh, in_specs=placed, out_specs=P("band", "grid", None), check_vma=False
    )
```

```python
import jax
import jax.numpy as jnp
import numpy as np
from jax import lax
from jax.experimental import pallas as pl
from jax.experimental.pallas import tpu as pltpu
from jax.sharding import PartitionSpec as P

N = 48
HALF = N // 2
PLANE = N * N
COLS = PLANE // 2
STOPS = 3
PAD = 8
SIDE = 3 * HALF + PAD
MESH = pl.DeviceIdType.MESH
CUTS = [(0, 256), (256, 256), (512, 256), (768, 256), (1024, 128)]


def cas(product, length):
    angle = (product % length) * (2.0 * np.pi / length)
    return np.cos(angle) + np.sin(angle)


def tables():
    i, h = np.arange(N), np.arange(HALF)
    along_z = np.tile(cas(i[:, None] * i[None, :], N), (1, HALF))
    even = cas(2 * h[:, None] * h[None, :], N)
    odd = cas(h[:, None] * (2 * h[None, :] + 1), N)
    along_y = np.stack([np.repeat(m, N, axis=1) for m in (even, odd, odd.T)])
    square = np.where(i <= HALF, i, i - N).astype(np.float64) ** 2
    order = np.concatenate([i[0::2], i[1::2]])
    total = square[:, None, None] + square[order][None, :, None] + square[None, None, :]
    coulomb = np.where(total > 0, 24.0 * 24.0 / np.pi / np.where(total > 0, total, 1.0), 0.0)
    coulomb = coulomb.reshape(N, PLANE) * (-0.25 / N**3)
    along_x = cas(i[:, None] * i[None, :], N)
    x_high = along_x.astype(np.float32).astype(jnp.bfloat16)
    x_low = (along_x - x_high.astype(np.float64)).astype(np.float32).astype(jnp.bfloat16)
    there, back = [], []
    for place in range(2):
        halves = [slice(s * HALF, (s + 1) * HALF) for s in (place, 1 - place)]
        pad = np.zeros((N, PAD), x_high.dtype)
        there.append(
            np.concatenate(
                [b for s in halves for b in (x_high[:, s], x_high[:, s], x_low[:, s], pad)], axis=1
            )
        )
        high, low = (np.concatenate([m[s] for s in halves]) for m in (x_high, x_low))
        back.append(np.concatenate([high, high, low], axis=1))
    return (
        along_z.astype(np.float32),
        along_y.astype(np.float32),
        np.stack(there),
        np.stack(back),
        coulomb.astype(np.float32),
    )


def split(value):
    high = value.astype(jnp.bfloat16)
    return high, (value - high.astype(jnp.float32)).astype(jnp.bfloat16)


def split32(value):
    high = value.astype(jnp.bfloat16).astype(jnp.float32)
    return high, value - high


def dot(a, b):
    return jnp.dot(a, b, preferred_element_type=jnp.float32)


def kernel(
    psi, occ, along_z, along_y, there, back, coulomb,
    out, buf, w_high, w_low, slabs, lhs, xrhs, acc, send, recv, out_send, out_recv,
):
    band, grid = lax.axis_index("band"), lax.axis_index("grid")
    devices = lax.axis_size("band")
    left = {"band": lax.rem(band + devices - 1, devices), "grid": grid}
    right = {"band": lax.rem(band + 1, devices), "grid": grid}
    across = {"band": band, "grid": 1 - grid}
    odd = lax.rem(band, 2) == 1

    barrier = pltpu.get_barrier_semaphore()
    for device in (across, right):
        pl.semaphore_signal(barrier, inc=1, device_id=device, device_id_type=MESH)

    def root(k):
        return jnp.sqrt(jnp.full((1, 128), occ[k], jnp.float32))

    for k in range(2):
        factor = root(k)
        for start in range(0, PLANE, 128):
            at = slice(start, start + 128)
            buf[0, k, 0, :, at] = psi[k, :, at] * factor

    def copy(number, k, source, target, device):
        return pltpu.make_async_remote_copy(
            src_ref=buf.at[source[0], k, source[1]],
            dst_ref=buf.at[target[0], k, target[1]],
            send_sem=send.at[number, k],
            recv_sem=recv.at[target[0], target[1], k],
            device_id=device,
            device_id_type=MESH,
        )

    swap = [copy(0, k, (0, 0), (0, 1), across) for k in (1 - grid, grid)]
    own = [copy(1, k, (0, 0), (1, 0), left) for k in range(2)]
    own_on = [copy(2, k, (1, 0), (2, 0), left) for k in range(2)]
    other = [copy(3, k, (0, 1), (1, 1), left) for k in range(2)]
    other_on = [copy(4, k, (1, 1), (2, 1), left) for k in range(2)]
    other_swap = [copy(5, k, (2, 0), (2, 1), across) for k in range(2)]

    def start(copies):
        for c in copies:
            c.start()

    def arrived(copies):
        for c in copies:
            c.wait_recv()

    def build(m):
        @pl.loop(0, HALF)
        def _(y):
            rows = pl.ds(pl.multiple_of(y * N, 16), N)
            high, low = split(along_z[...] * along_y[m, pl.ds(y, 1), :])
            w_high[m, rows, :] = high
            w_low[m, rows, :] = low

    def forward(stop, side):
        for first in range(0, COLS, 128):
            cols = [slice(s, s + 128) for s in (first, COLS + first)]
            low_y, high_y = (
                jnp.concatenate([buf[0, grid, side, :, c] * buf[stop, k, side, :, c] for k in range(2)])
                for c in cols
            )
            for parity, value in enumerate((low_y + high_y, low_y - high_y)):
                slabs[parity, :N, cols[0]], slabs[parity, N:, cols[0]] = split(value)
        for parity in range(2):
            for first, size in CUTS:
                cut = slice(first, first + size)
                both = dot(slabs[parity], w_high[parity, :, cut])
                value = both[:N] + both[N:] + dot(slabs[parity, :N, :], w_low[parity, :, cut])
                high, low = split32(value)
                to = slice(parity * COLS + first, parity * COLS + first + size)
                for k in range(2):
                    rows = slice(k * HALF, (k + 1) * HALF)
                    pad = jnp.zeros((PAD, size), jnp.float32)
                    block = jnp.concatenate([high[rows], low[rows], high[rows], pad])
                    xrhs[stop, k, side * SIDE : (side + 1) * SIDE, to] = block.astype(jnp.bfloat16)

    def finish(stop):
        for parity in range(2):
            for first, size in CUTS:
                at = slice(parity * COLS + first, parity * COLS + first + size)
                for k in range(2):
                    work = dot(there[grid], xrhs[stop, k, :, at]) * coulomb[:, at]
                    high, low = split(work)
                    work = dot(back[grid], jnp.concatenate([high, low, high]))
                    high, low = split(work)
                    lhs[parity, k * N : (k + 1) * N, first : first + size] = high
                    lhs[parity, (k + 2) * N : (k + 3) * N, first : first + size] = low

        def yz(which, parity, cut):
            both = dot(lhs[parity], w_high[which, :, cut])
            return both[: 2 * N] + both[2 * N :] + dot(lhs[parity, : 2 * N, :], w_low[which, :, cut])

        sent = []
        scale = 1.0 / root(grid)[:, :1] if stop == STOPS - 1 else None
        for first, size in CUTS:
            cols = [slice(s, s + size) for s in (first, COLS + first)]
            even, odd_y = yz(0, 0, cols[0]), yz(2, 1, cols[0])
            for at, value in zip(cols, (even + odd_y, even - odd_y)):
                for side in range(2):
                    rows = slice(side * HALF, (side + 1) * HALF)
                    term = sum(
                        value[k * N + side * HALF : k * N + (side + 1) * HALF] * buf[stop, k, side, :, at]
                        for k in range(2)
                    )
                    if stop > 0:
                        term = term + acc[rows, at]
                    if scale is None:
                        acc[rows, at] = term
                    elif side == 0:
                        out[grid, :, at] = term * scale
                    else:
                        acc[rows, at] = term * scale
                if scale is not None:
                    sent.append(
                        pltpu.make_async_remote_copy(
                            src_ref=acc.at[pl.ds(HALF, HALF), pl.ds(at.start, size)],
                            dst_ref=out.at[grid, :, pl.ds(at.start, size)],
                            send_sem=out_send.at[len(sent)],
                            recv_sem=out_recv.at[len(sent)],
                            device_id=across,
                            device_id_type=MESH,
                        )
                    )
                    sent[-1].start()
        return sent

    pl.semaphore_wait(barrier, 2)
    start(swap)
    start(own)
    build(0)
    build(1)
    forward(0, 0)
    arrived(own)
    start(own_on)
    forward(1, 0)
    build(2)
    arrived(swap)
    start(other)
    arrived(own_on)

    @pl.when(odd)
    def _():
        start(other_swap)

    forward(0, 1)
    finish(0)
    forward(2, 0)
    arrived(other)

    @pl.when(odd)
    def _():
        start(other_on)

    forward(1, 1)
    finish(1)
    arrived(other_on)
    forward(2, 1)
    sent = finish(2)
    for c in swap + own + own_on + other:
        c.wait_send()

    @pl.when(odd)
    def _():
        for c in other_on + other_swap:
            c.wait_send()

    for c in sent:
        c.wait()


def per_device(orbitals, occupation):
    count, slab, plane = orbitals.shape
    vmem = pl.BlockSpec(memory_space=pltpu.VMEM)
    return pl.pallas_call(
        kernel,
        out_shape=jax.ShapeDtypeStruct((count, slab, plane), jnp.float32),
        in_specs=[vmem, pl.BlockSpec(memory_space=pltpu.SMEM)] + [vmem] * 5,
        out_specs=vmem,
        scratch_shapes=[
            pltpu.VMEM((STOPS, count, 2, slab, plane), jnp.float32),
            pltpu.VMEM((3, COLS, COLS), jnp.bfloat16),
            pltpu.VMEM((3, COLS, COLS), jnp.bfloat16),
            pltpu.VMEM((2, 2 * N, COLS), jnp.bfloat16),
            pltpu.VMEM((2, 4 * N, COLS), jnp.bfloat16),
            pltpu.VMEM((STOPS, count, 2 * SIDE, plane), jnp.bfloat16),
            pltpu.VMEM((N, plane), jnp.float32),
            pltpu.SemaphoreType.DMA((6, count)),
            pltpu.SemaphoreType.DMA((STOPS, 2, count)),
            pltpu.SemaphoreType.DMA((2 * len(CUTS),)),
            pltpu.SemaphoreType.DMA((2 * len(CUTS),)),
        ],
        compiler_params=pltpu.CompilerParams(
            vmem_limit_bytes=50 << 20, collective_id=0, has_side_effects=True
        ),
    )(orbitals, occupation, *[jnp.asarray(t) for t in tables()])


def solution(mesh):
    placed = (P("band", "grid", None), P("band"))
    return jax.shard_map(
        per_device, mesh=mesh, in_specs=placed, out_specs=P("band", "grid", None), check_vma=False
    )
```

```python
import jax
import jax.numpy as jnp
import numpy as np
from jax import lax
from jax.experimental import pallas as pl
from jax.experimental.pallas import tpu as pltpu
from jax.sharding import PartitionSpec as P

N = 48
HALF = N // 2
PLANE = N * N
COLS = PLANE // 2
STOPS = 3
PAD = 8
SIDE = 3 * HALF + PAD
MESH = pl.DeviceIdType.MESH
CUTS = [(0, 256), (256, 256), (512, 256), (768, 256), (1024, 128)]


def cas(product, length):
    angle = (product % length) * (2.0 * np.pi / length)
    return np.cos(angle) + np.sin(angle)


def tables():
    i, h = np.arange(N), np.arange(HALF)
    along_z = np.tile(cas(i[:, None] * i[None, :], N), (1, HALF))
    even = cas(2 * h[:, None] * h[None, :], N)
    odd = cas(h[:, None] * (2 * h[None, :] + 1), N)
    along_y = np.stack([np.repeat(m, N, axis=1) for m in (even, odd, odd.T)])
    square = np.where(i <= HALF, i, i - N).astype(np.float64) ** 2
    order = np.concatenate([i[0::2], i[1::2]])
    total = square[:, None, None] + square[order][None, :, None] + square[None, None, :]
    coulomb = np.where(total > 0, 24.0 * 24.0 / np.pi / np.where(total > 0, total, 1.0), 0.0)
    coulomb = coulomb.reshape(N, PLANE) * (-0.25 / N**3)
    along_x = cas(i[:, None] * i[None, :], N)
    x_high = along_x.astype(np.float32).astype(jnp.bfloat16)
    x_low = (along_x - x_high.astype(np.float64)).astype(np.float32).astype(jnp.bfloat16)
    there, back = [], []
    for place in range(2):
        halves = [slice(s * HALF, (s + 1) * HALF) for s in (place, 1 - place)]
        pad = np.zeros((N, PAD), x_high.dtype)
        there.append(
            np.concatenate(
                [b for s in halves for b in (x_high[:, s], x_high[:, s], x_low[:, s], pad)], axis=1
            )
        )
        high, low = (np.concatenate([m[s] for s in halves]) for m in (x_high, x_low))
        back.append(np.concatenate([high, high, low], axis=1))
    return (
        along_z.astype(np.float32),
        along_y.astype(np.float32),
        np.stack(there),
        np.stack(back),
        coulomb.astype(np.float32),
    )


def split(value):
    high = value.astype(jnp.bfloat16)
    return high, (value - high.astype(jnp.float32)).astype(jnp.bfloat16)


def split32(value):
    high = value.astype(jnp.bfloat16).astype(jnp.float32)
    return high, value - high


def dot(a, b):
    return jnp.dot(a, b, preferred_element_type=jnp.float32)


def kernel(
    occ, psi_in, z_in, y_in, there_in, back_in, coulomb_in,
    out, psi, along_z, along_y, there, back, coulomb,
    buf, w_high, w_low, slabs, lhs, xrhs, acc, load, send, recv, out_send, out_recv,
):
    sources = (psi_in, z_in, y_in, there_in, back_in, coulomb_in)
    targets = (psi, along_z, along_y, there, back, coulomb)
    loads = [pltpu.make_async_copy(a, b, load.at[i]) for i, (a, b) in enumerate(zip(sources, targets))]
    for c in loads:
        c.start()
    band, grid = lax.axis_index("band"), lax.axis_index("grid")
    devices = lax.axis_size("band")
    left = {"band": lax.rem(band + devices - 1, devices), "grid": grid}
    right = {"band": lax.rem(band + 1, devices), "grid": grid}
    across = {"band": band, "grid": 1 - grid}
    odd = lax.rem(band, 2) == 1

    barrier = pltpu.get_barrier_semaphore()
    for device in (across, right):
        pl.semaphore_signal(barrier, inc=1, device_id=device, device_id_type=MESH)

    def root(k):
        return jnp.sqrt(jnp.full((1, 128), occ[k], jnp.float32))

    loads[0].wait()
    for k in range(2):
        factor = root(k)
        for start in range(0, PLANE, 128):
            at = slice(start, start + 128)
            buf[0, k, 0, :, at] = psi[k, :, at] * factor

    def copy(number, k, source, target, device):
        return pltpu.make_async_remote_copy(
            src_ref=buf.at[source[0], k, source[1]],
            dst_ref=buf.at[target[0], k, target[1]],
            send_sem=send.at[number, k],
            recv_sem=recv.at[target[0], target[1], k],
            device_id=device,
            device_id_type=MESH,
        )

    swap = [copy(0, k, (0, 0), (0, 1), across) for k in (1 - grid, grid)]
    own = [copy(1, k, (0, 0), (1, 0), left) for k in range(2)]
    own_on = [copy(2, k, (1, 0), (2, 0), left) for k in range(2)]
    other = [copy(3, k, (0, 1), (1, 1), left) for k in range(2)]
    other_on = [copy(4, k, (1, 1), (2, 1), left) for k in range(2)]
    other_swap = [copy(5, k, (2, 0), (2, 1), across) for k in range(2)]

    def start(copies):
        for c in copies:
            c.start()

    def arrived(copies):
        for c in copies:
            c.wait_recv()

    def build(m):
        @pl.loop(0, HALF)
        def _(y):
            rows = pl.ds(pl.multiple_of(y * N, 16), N)
            high, low = split(along_z[...] * along_y[m, pl.ds(y, 1), :])
            w_high[m, rows, :] = high
            w_low[m, rows, :] = low

    def forward(*parts):
        rows = N * len(parts)
        for first in range(0, COLS, 128):
            cols = [slice(s, s + 128) for s in (first, COLS + first)]
            low_y, high_y = (
                jnp.concatenate(
                    [
                        buf[0, grid, side, :, c] * buf[stop, k, side, :, c]
                        for stop, side in parts
                        for k in range(2)
                    ]
                )
                for c in cols
            )
            for parity, value in enumerate((low_y + high_y, low_y - high_y)):
                slabs[parity, :rows, cols[0]], slabs[parity, rows:, cols[0]] = split(value)
        for parity in range(2):
            for first, size in CUTS:
                cut = slice(first, first + size)
                both = dot(slabs[parity], w_high[parity, :, cut])
                value = both[:rows] + both[rows:] + dot(slabs[parity, :rows, :], w_low[parity, :, cut])
                high, low = split32(value)
                to = slice(parity * COLS + first, parity * COLS + first + size)
                pad = jnp.zeros((PAD, size), jnp.float32)
                for n, (stop, side) in enumerate(parts):
                    for k in range(2):
                        at = slice((2 * n + k) * HALF, (2 * n + k + 1) * HALF)
                        block = jnp.concatenate([high[at], low[at], high[at], pad])
                        xrhs[stop, k, side * SIDE : (side + 1) * SIDE, to] = block.astype(jnp.bfloat16)

    def finish(stops, hook=None):
        pairs = [(stop, k) for stop in stops for k in range(2)]
        rows = N * len(pairs)
        for first in range(0, PLANE, 256):
            at = slice(first, first + 256)
            for n, (stop, k) in enumerate(pairs):
                work = dot(there[grid], xrhs[stop, k, :, at]) * coulomb[:, at]
                high, low = split(work)
                work = dot(back[grid], jnp.concatenate([high, low, high]))
                high, low = split(work)
                lhs[n * N : (n + 1) * N, at] = high
                lhs[rows + n * N : rows + (n + 1) * N, at] = low

        def yz(which, parity, cut):
            half = slice(parity * COLS, (parity + 1) * COLS)
            both = dot(lhs[: 2 * rows, half], w_high[which, :, cut])
            return both[:rows] + both[rows:] + dot(lhs[:rows, half], w_low[which, :, cut])

        last = STOPS - 1 in stops
        scale = 1.0 / root(grid)[:, :1] if last else None
        sent = []
        for number, (first, size) in enumerate(CUTS):
            cols = [slice(s, s + size) for s in (first, COLS + first)]
            even, odd_y = yz(0, 0, cols[0]), yz(2, 1, cols[0])
            for at, value in zip(cols, (even + odd_y, even - odd_y)):
                for side in range(2):
                    part = slice(side * HALF, (side + 1) * HALF)
                    term = sum(
                        value[n * N + side * HALF : n * N + (side + 1) * HALF] * buf[stop, k, side, :, at]
                        for n, (stop, k) in enumerate(pairs)
                    )
                    if 0 not in stops:
                        term = term + acc[part, at]
                    if not last:
                        acc[part, at] = term
                    elif side == 0:
                        out[grid, :, at] = term * scale
                    else:
                        acc[part, at] = term * scale
                if last:
                    sent.append(
                        pltpu.make_async_remote_copy(
                            src_ref=acc.at[pl.ds(HALF, HALF), pl.ds(at.start, size)],
                            dst_ref=out.at[grid, :, pl.ds(at.start, size)],
                            send_sem=out_send.at[len(sent)],
                            recv_sem=out_recv.at[len(sent)],
                            device_id=across,
                            device_id_type=MESH,
                        )
                    )
                    sent[-1].start()
            if hook is not None and number == 2:
                hook()
        return sent

    def pass_other():
        arrived(other)

        @pl.when(odd)
        def _():
            start(other_on)

    pl.semaphore_wait(barrier, 2)
    start(swap)
    start(own)
    loads[1].wait()
    loads[2].wait()
    build(0)
    build(1)
    build(2)
    for c in loads[3:]:
        c.wait()
    arrived(own)
    start(own_on)
    forward((0, 0), (1, 0))
    arrived(swap)
    start(other)
    arrived(own_on)

    @pl.when(odd)
    def _():
        start(other_swap)

    forward((0, 1), (2, 0))
    finish([0], pass_other)
    arrived(other_on)
    forward((1, 1), (2, 1))
    sent = finish([1, 2])
    for c in swap + own + own_on + other:
        c.wait_send()

    @pl.when(odd)
    def _():
        for c in other_on + other_swap:
            c.wait_send()

    for c in sent:
        c.wait()


def per_device(orbitals, occupation):
    count, slab, plane = orbitals.shape
    vmem = pl.BlockSpec(memory_space=pltpu.VMEM)
    operands = [orbitals] + [jnp.asarray(t) for t in tables()]
    return pl.pallas_call(
        kernel,
        out_shape=jax.ShapeDtypeStruct((count, slab, plane), jnp.float32),
        in_specs=[pl.BlockSpec(memory_space=pltpu.SMEM)] + [pl.BlockSpec(memory_space=pltpu.HBM)] * 6,
        out_specs=vmem,
        scratch_shapes=[pltpu.VMEM(t.shape, t.dtype) for t in operands]
        + [
            pltpu.VMEM((STOPS, count, 2, slab, plane), jnp.float32),
            pltpu.VMEM((3, COLS, COLS), jnp.bfloat16),
            pltpu.VMEM((3, COLS, COLS), jnp.bfloat16),
            pltpu.VMEM((2, 4 * N, COLS), jnp.bfloat16),
            pltpu.VMEM((8 * N, PLANE), jnp.bfloat16),
            pltpu.VMEM((STOPS, count, 2 * SIDE, plane), jnp.bfloat16),
            pltpu.VMEM((N, plane), jnp.float32),
            pltpu.SemaphoreType.DMA((6,)),
            pltpu.SemaphoreType.DMA((6, count)),
            pltpu.SemaphoreType.DMA((STOPS, 2, count)),
            pltpu.SemaphoreType.DMA((2 * len(CUTS),)),
            pltpu.SemaphoreType.DMA((2 * len(CUTS),)),
        ],
        compiler_params=pltpu.CompilerParams(
            vmem_limit_bytes=50 << 20, collective_id=0, has_side_effects=True
        ),
    )(occupation, *operands)


def solution(mesh):
    placed = (P("band", "grid", None), P("band"))
    return jax.shard_map(
        per_device, mesh=mesh, in_specs=placed, out_specs=P("band", "grid", None), check_vma=False
    )
```
